32 devices in a mesh: member: 4 (over z), space: 4 (over y, x), group: 2 (over core).
Axes of the slice: x: 2, y: 2, z: 4, core: 2. Of those that a mesh axis runs over, the one named last changes fastest.
Arguments:
- ensemble: bfloat16 [2, 512, 3, 16, 512], P('group', 'member', None, 'space'), may hold values from -6 to 6
- obs_index: int32 [2, 4, 4, 256], P('group', 'space'), may hold values from 0 to 511
- obs_value: float32 [2, 4, 4, 256], P('group', 'space', 'member'), may hold values from -6 to 6
- obs_var: float32 [2, 4, 4, 256], P('group', 'space', 'member'), may hold values from 0.3 to 3
Outputs:
- analysis: bfloat16 [2, 512, 3, 16, 512], P('group', 'member', None, 'space')
The draws below stay inside these ranges and needn't reach their ends.
Inputs may be any that keep to these rules, and one draw needn't show every extreme that they name: `obs_index`: each entry names a cell of its region's tile, counted row by row over 128 columns; cells may repeat.
All inputs are finite; a program needn't handle non-finite values.
Results may differ from the reference program's by a relative error of at most 0.0075.
Values may be sent and summed in bfloat16 or wider, within the bound.
A program may use at most 64 MiB of HBM per device.

```python
import math
import jax
import jax.numpy as jnp
from jax import lax

MEMBERS = 512
MESH_WIDTH = 512
ROWS_DEV = 4
OBS = 256
STEPS = 2
NS_STEPS = 6
MESH_LATITUDES = 16
PATCH_DOWNWARD = 4
PATCH_ACROSS = 4
CELLS = 512
N_MEMBER = 4
N_GROUP = 2


def plant(drawn, rng, low, largest):
    spot = [jax.random.randint(jax.random.fold_in(rng, axis), (), 0, length) for axis, length in enumerate(drawn.shape)]
    main_axis = drawn.shape.index(max(drawn.shape))
    neighbour = spot[:main_axis] + [(spot[main_axis] + 1) % drawn.shape[main_axis]] + spot[main_axis + 1:]
    return drawn.at[tuple(spot)].set(low).at[tuple(neighbour)].set(largest)


def block_scale(key, dims, cuts, least, top_value):
    def one(position, blocks):
        draws = jax.random.uniform(jax.random.fold_in(jax.random.fold_in(key, 6), position), (blocks,), jnp.float32, least / len(cuts), top_value / len(cuts))
        return jnp.repeat(jnp.exp(draws), dims[position] // blocks).reshape((-1,) + (1,) * (len(dims) - position - 1))

    gain = one(*cuts[0])
    for cut in cuts[1:]:
        gain = gain * one(*cut)
    return gain


def centred(stream_key, shape, width, bound, cuts=(), kind=jnp.bfloat16):
    array = jax.random.normal(stream_key, shape, jnp.float32) * width
    if len(cuts) > 0:
        array = block_scale(stream_key, shape, cuts, -0.22, 0.18) * array
    return jnp.clip(array, min=-bound, max=bound).astype(kind)


def setup_inputs(seed: int = 0) -> dict:
    key_list = jax.random.split(jax.random.key(seed), 5)
    return {
        "ensemble": centred(key_list[0], (N_GROUP, MEMBERS, 3, MESH_LATITUDES, MESH_WIDTH), 1.0, 6.0, ((0, 2), (1, 4), (3, 4))),
        "obs_index": plant(jax.random.randint(key_list[1], (N_GROUP, PATCH_DOWNWARD, PATCH_ACROSS, OBS), 0, CELLS), jax.random.fold_in(key_list[1], 1), 0, CELLS - 1).astype(jnp.int32),
        "obs_value": centred(key_list[2], (N_GROUP, PATCH_DOWNWARD, PATCH_ACROSS, OBS), 1.0, 6.0, ((0, 2), (1, 4), (2, 4)), jnp.float32),
        "obs_var": jnp.clip(jnp.exp(math.log(3.0) - 2.3025851 * jax.random.uniform(key_list[3], (N_GROUP, PATCH_DOWNWARD, PATCH_ACROSS, OBS), jnp.float32) ** block_scale(key_list[3], (N_GROUP, PATCH_DOWNWARD, PATCH_ACROSS, OBS), ((0, 2), (1, 4), (2, 4)), -0.2, 0.2)), 0.3, 3.0),
    }


time_step = 0.4
coriolis = 0.3

def tendency(height, northward, eastward):
    d_height = -(0.5 * (jnp.roll(eastward, -1, -1) - jnp.roll(eastward, 1, -1)) + 0.5 * (northward[..., 2:, :] - northward[..., :-2, :]))
    d_north = -0.5 * (height[..., 2:, :] - height[..., :-2, :]) - coriolis * eastward
    d_east = -0.5 * (jnp.roll(height, -1, -1) - jnp.roll(height, 1, -1))[..., 1:-1, :] + coriolis * northward[..., 1:-1, :]
    return jnp.stack((d_height, d_north, d_east), axis=1)

def wrap_rows(section):
    return jnp.concatenate((section[..., -1:, :], section, section[..., :1, :]), axis=-2)

def segment_rates(present_states):
    padded = wrap_rows(present_states[:, 0:2])
    return tendency(padded[:, 0], padded[:, 1], present_states[:, 2])

def predicted_patch_slab(patch_slab):
    present_states = patch_slab.astype(jnp.float32)
    for repeat in range(STEPS):
        segment_one = present_states + time_step * segment_rates(present_states)
        segment_two = 0.75 * present_states + 0.25 * (segment_one + time_step * segment_rates(segment_one))
        present_states = present_states / 3.0 + 2.0 / 3.0 * (segment_two + time_step * segment_rates(segment_two))
    return present_states.astype(jnp.bfloat16)

def region_weights(sampled, values, variances):
    sample_states = sampled.shape[0]
    high = lax.Precision.HIGHEST
    mean_obs = lax.optimization_barrier(jnp.mean(sampled, axis=0))
    spread = sampled - mean_obs
    scaled = spread / variances
    identity = jnp.eye(sample_states, dtype=jnp.float32)
    gram = (sample_states - 1.0) * identity + jnp.dot(scaled, spread.T, precision=high, preferred_element_type=jnp.float32)
    drive = jnp.dot(scaled, values - mean_obs, precision=high, preferred_element_type=jnp.float32)
    norm_f = jnp.sqrt(jnp.sum(gram * gram))
    upper_part = gram / norm_f
    lower_part = identity
    for repeat in range(NS_STEPS):
        step_matrix = 1.5 * identity - 0.5 * jnp.dot(lower_part, upper_part, precision=high, preferred_element_type=jnp.float32)
        upper_part = jnp.dot(upper_part, step_matrix, precision=high, preferred_element_type=jnp.float32)
        lower_part = jnp.dot(step_matrix, lower_part, precision=high, preferred_element_type=jnp.float32)
    root = lower_part / jnp.sqrt(norm_f)
    centre = jnp.dot(root, jnp.dot(root, drive, precision=high, preferred_element_type=jnp.float32), precision=high, preferred_element_type=jnp.float32)
    return (math.sqrt(sample_states - 1.0) * root + centre[:, None]).astype(jnp.bfloat16)

def blend(deviation, tile_mean, corner):
    sample_states, fields, latitude_number, longitude_number = deviation.shape
    half_rows = latitude_number // 2
    half_cols = longitude_number // 2
    row_weight = jnp.abs((jnp.arange(latitude_number, dtype=jnp.float32) + 0.5) / latitude_number - 0.5)
    col_weight = jnp.abs((jnp.arange(longitude_number, dtype=jnp.float32) + 0.5) / longitude_number - 0.5)
    bands = []
    for row_half in range(2):
        pieces = []
        row_part = slice(row_half * half_rows, (row_half + 1) * half_rows)
        row_step = -1 if row_half == 0 else 1
        for col_half in range(2):
            col_part = slice(col_half * half_cols, (col_half + 1) * half_cols)
            col_step = -1 if col_half == 0 else 1
            quarter = deviation[:, :, row_part, col_part].reshape(sample_states, -1)
            row_near = row_weight[row_part][:, None]
            col_near = col_weight[col_part][None, :]
            summed = tile_mean[:, row_part, col_part]
            terms = ((1, 1, (1.0 - row_near) * (1.0 - col_near)), (1 + row_step, 1, row_near * (1.0 - col_near)), (1, 1 + col_step, (1.0 - row_near) * col_near), (1 + row_step, 1 + col_step, row_near * col_near))
            for row_pick, col_pick, factor in terms:
                product = lax.dot_general(corner[row_pick, col_pick], quarter, (((0,), (0,)), ((), ())), preferred_element_type=jnp.float32)
                summed = summed + factor * product.reshape(sample_states, fields, half_rows, half_cols)
            pieces.append(summed)
        bands.append(jnp.concatenate(pieces, axis=3))
    return jnp.concatenate(bands, axis=2).astype(jnp.bfloat16)

def reference(ensemble, obs_index, obs_value, obs_var):
    sample_states = MEMBERS
    latitude_number = ROWS_DEV
    longitude_number = MESH_WIDTH // PATCH_ACROSS
    patch_sequence = PATCH_DOWNWARD * PATCH_ACROSS
    outputs = []
    for stream in range(2):
        patch_slabs = ensemble[stream].reshape(N_MEMBER, sample_states // N_MEMBER, 3, MESH_LATITUDES, MESH_WIDTH)
        predicted_states = lax.map(predicted_patch_slab, patch_slabs).reshape(sample_states, 3, MESH_LATITUDES, MESH_WIDTH)
        subdomain_parts = predicted_states.reshape(sample_states, 3, PATCH_DOWNWARD, latitude_number, PATCH_ACROSS, longitude_number).transpose(2, 4, 0, 1, 3, 5).reshape(patch_sequence, sample_states, 3, latitude_number, longitude_number)

        def one_region(inputs):
            tile, index_row, value_row, var_row = inputs
            sampled = jnp.take(tile[:, 0].reshape(sample_states, -1), index_row, axis=1).astype(jnp.float32)
            return region_weights(sampled, value_row, var_row)
        weights = lax.map(one_region, (subdomain_parts, obs_index[stream].reshape(patch_sequence, OBS), obs_value[stream].reshape(patch_sequence, OBS), obs_var[stream].reshape(patch_sequence, OBS)))
        weights = weights.reshape(PATCH_DOWNWARD, PATCH_ACROSS, sample_states, sample_states)

        def one_blend(inputs):
            tile, place = inputs
            band = place // PATCH_ACROSS
            column = place % PATCH_ACROSS
            row_ids = (band + jnp.arange(-1, 2, dtype=jnp.int32)) % PATCH_DOWNWARD
            col_ids = (column + jnp.arange(-1, 2, dtype=jnp.int32)) % PATCH_ACROSS
            corner = weights[row_ids][:, col_ids]
            tile_mean = lax.optimization_barrier(jnp.mean(tile.astype(jnp.float32), axis=0))
            deviation = (tile.astype(jnp.float32) - tile_mean).astype(jnp.bfloat16)
            return blend(deviation, tile_mean, corner)
        analysed = lax.map(one_blend, (subdomain_parts, jnp.arange(patch_sequence, dtype=jnp.int32)))
        outputs.append(analysed.reshape(PATCH_DOWNWARD, PATCH_ACROSS, sample_states, 3, latitude_number, longitude_number).transpose(2, 3, 0, 4, 1, 5).reshape(sample_states, 3, MESH_LATITUDES, MESH_WIDTH))
    return jnp.stack(outputs)
```

```python
import math

import jax
import jax.numpy as jnp
from jax import lax
from jax.sharding import PartitionSpec as P

STEPS = 2
NS_STEPS = 6
TIME_STEP = 0.4
CORIOLIS = 0.3
HIGH = lax.Precision.HIGHEST


def rates(state):
    height, northward, eastward = state

    def d_col(f):
        return 0.5 * (jnp.roll(f, -1, -1) - jnp.roll(f, 1, -1))

    def d_row(f):
        return 0.5 * (jnp.roll(f, -1, 0) - jnp.roll(f, 1, 0))

    return (
        -(d_col(eastward) + d_row(northward)),
        -d_row(height) - CORIOLIS * eastward,
        -d_col(height) + CORIOLIS * northward,
    )


def forecast(block):
    now = tuple(block[f].astype(jnp.float32) for f in range(3))
    for _ in range(STEPS):
        one = tuple(a + TIME_STEP * r for a, r in zip(now, rates(now)))
        two = tuple(
            0.75 * a + 0.25 * (b + TIME_STEP * r) for a, b, r in zip(now, one, rates(one))
        )
        now = tuple(
            a / 3.0 + 2.0 / 3.0 * (b + TIME_STEP * r) for a, b, r in zip(now, two, rates(two))
        )
    return jnp.stack(now).astype(jnp.bfloat16)


def mm(a, b, dims=(((1,), (0,)), ((), ()))):
    return lax.dot_general(a, b, dims, precision=HIGH, preferred_element_type=jnp.float32)


def region_weights(sampled, values, variances):
    members, obs = sampled.shape
    mean_obs = jnp.mean(sampled, axis=0)
    inv = lax.rsqrt(variances)
    basis = (sampled - mean_obs) * inv
    innovation = (values - mean_obs) * inv
    base = members - 1.0
    identity = jnp.eye(obs, dtype=jnp.float32)
    cross = mm(basis, basis, (((0,), (0,)), ((), ())))
    trace = jnp.sum(cross * identity)
    norm_f = jnp.sqrt(members * base * base + 2.0 * base * trace + jnp.sum(cross * cross))
    m = base / norm_f
    l = 1.0
    ym = identity / norm_f
    pm = cross / norm_f + m * identity
    yl = None
    pl_ = None
    for step in range(NS_STEPS):
        s = 1.5 - 0.5 * m
        if step == 0:
            yl, pl_ = -0.5 * ym, 1.5 * identity - 0.5 * pm
        else:
            both = mm(jnp.concatenate([ym, pm]), pl_)
            yl, pl_ = s * yl - 0.5 * both[:obs], 1.5 * pl_ - 0.5 * both[obs:]
        l = s * l
        if step < NS_STEPS - 1:
            square = mm(pm, pm)
            h = (2.25 - 1.5 * m + 0.25 * m * m) * identity + (0.25 * m - 1.5) * pm + 0.25 * square
            both = mm(jnp.concatenate([ym, pm - m * identity]), h)
            m = m * s * s
            ym, pm = both[:obs], both[obs:] + m * identity
    scale = 1.0 / jnp.sqrt(norm_f)
    gain = math.sqrt(base) * scale
    coeff = mm(pl_, mm(pl_, innovation[:, None])) * (scale * scale)
    centre = mm(basis, coeff)
    spread = mm(mm(basis, yl * gain), basis, (((1,), (1,)), ((), ())))
    eye = jnp.eye(members, dtype=jnp.float32)
    return (spread + (gain * l) * eye + centre).astype(jnp.bfloat16)


def per_device(ensemble, obs_index, obs_value, obs_var):
    space = lax.axis_size("space")
    groups = lax.axis_size("member")
    local, fields, rows, width = ensemble.shape[1:]
    regions = obs_index.shape[2]
    cols = width // regions
    members = local * groups
    block = ensemble[0].reshape(space, local // space, fields, rows, width)
    block = block.transpose(0, 2, 3, 1, 4)
    block = lax.all_to_all(block, "space", split_axis=0, concat_axis=0, tiled=True)
    block = block.transpose(1, 0, 2, 3, 4).reshape(fields, space * rows, local // space, width)
    ahead = forecast(block)
    back = ahead.reshape(fields, space, rows, local // space, width).transpose(1, 0, 2, 3, 4)
    back = lax.all_to_all(back, "space", split_axis=0, concat_axis=0, tiled=True)
    mine = back.transpose(1, 2, 0, 3, 4).reshape(fields, rows, local, width)
    everyone = lax.all_gather(mine, "member", axis=0, tiled=False)

    heights = mine[0].reshape(rows, local, regions, cols)
    index = obs_index[0, 0]
    cells = lax.broadcasted_iota(jnp.int32, (regions, rows, cols, index.shape[1]), 1) * cols
    cells = cells + lax.broadcasted_iota(jnp.int32, cells.shape, 2)
    pick = (cells == index[:, None, None, :]).astype(jnp.bfloat16)
    picked = jnp.einsum("rmbc,brcp->bmp", heights, pick, preferred_element_type=jnp.float32)
    sampled = lax.all_to_all(
        picked.astype(jnp.bfloat16), "member", split_axis=0, concat_axis=1, tiled=True
    )[0].astype(jnp.float32)
    weights = region_weights(sampled, obs_value[0, 0, 0], obs_var[0, 0, 0])
    weights = weights.reshape(members, groups, local).transpose(1, 0, 2)
    weights = lax.all_to_all(weights, "member", split_axis=0, concat_axis=0, tiled=True)
    up = [(i, (i + 1) % space) for i in range(space)]
    down = [(j, i) for i, j in up]
    above = lax.ppermute(weights, "space", up)
    below = lax.ppermute(weights, "space", down)
    near = (above, weights, below)

    full = everyone.astype(jnp.float32)
    mean = jnp.mean(full, axis=(0, 3))
    deviation = (full - mean[None, :, :, None, :]).astype(jnp.bfloat16)
    half_rows = rows // 2
    half = cols // 2
    deviation = jnp.roll(deviation, -half, -1)
    mean = jnp.roll(mean, -half, -1)
    row_weight = jnp.abs((jnp.arange(rows, dtype=jnp.float32) + 0.5) / rows - 0.5)
    far = (jnp.arange(cols, dtype=jnp.float32) + 0.5) / cols
    bands = []
    for row_half in range(2):
        part = slice(row_half * half_rows, (row_half + 1) * half_rows)
        r = row_weight[part][:, None, None]
        own, other = near[1], near[2 * row_half]
        pieces = []
        for b in range(regions):
            nxt = (b + 1) % regions
            span = slice(b * cols, (b + 1) * cols)
            stack = jnp.concatenate([own[b], own[nxt], other[b], other[nxt]], axis=1)
            quarter = deviation[:, :, part, :, span]
            product = lax.dot_general(
                stack.reshape(groups, local, 4 * local),
                quarter,
                (((0, 1), (0, 3)), ((), ())),
                preferred_element_type=jnp.float32,
            ).reshape(4, local, fields, half_rows, cols)
            product = product.transpose(0, 2, 3, 1, 4)
            summed = mean[:, part, None, span] + (
                (1.0 - r) * ((1.0 - far) * product[0] + far * product[1])
                + r * ((1.0 - far) * product[2] + far * product[3])
            )
            pieces.append(summed.astype(jnp.bfloat16))
        bands.append(jnp.concatenate(pieces, axis=-1))
    out = jnp.roll(jnp.concatenate(bands, axis=1), half, -1)
    return out.transpose(2, 0, 1, 3)[None]


def solution(mesh):
    return jax.shard_map(
        per_device,
        mesh=mesh,
        in_specs=(
            P("group", "member", None, "space", None),
            P("group", "space", None, None),
            P("group", "space", "member", None),
            P("group", "space", "member", None),
        ),
        out_specs=P("group", "member", None, "space", None),
        check_vma=False,
    )
```

```python
import math

import jax
import jax.numpy as jnp
from jax import lax
from jax.experimental import pallas as pl
from jax.experimental.pallas import tpu as pltpu
from jax.sharding import PartitionSpec as P

STEPS = 2
NS_STEPS = 6
TIME_STEP = 0.4
CORIOLIS = 0.3
HIGH = lax.Precision.HIGHEST


def forecast_kernel(block_ref, out_ref, now_ref, one_ref, two_ref):
    space, fields, rows, local, width = block_ref.shape
    total = space * rows

    for f in range(fields):
        for r in range(total):
            now_ref[f, r] = block_ref[r // rows, f, r % rows].astype(jnp.float32)

    def d_col(f):
        return 0.5 * (pltpu.roll(f, width - 1, 1) - pltpu.roll(f, 1, 1))

    def segment(source_ref, combine):
        def row(r, carry):
            up = lax.rem(r + 1, total)
            down = lax.rem(r + total - 1, total)
            h, v, u = source_ref[0, r], source_ref[1, r], source_ref[2, r]
            d_h = -(d_col(u) + 0.5 * (source_ref[1, up] - source_ref[1, down]))
            d_v = -0.5 * (source_ref[0, up] - source_ref[0, down]) - CORIOLIS * u
            d_u = -d_col(h) + CORIOLIS * v
            for f, (value, rate) in enumerate(((h, d_h), (v, d_v), (u, d_u))):
                combine(f, r, value + TIME_STEP * rate)
            return carry

        lax.fori_loop(0, total, row, 0)

    def set_one(f, r, value):
        one_ref[f, r] = value

    def set_two(f, r, value):
        two_ref[f, r] = 0.75 * now_ref[f, r] + 0.25 * value

    def set_now(f, r, value):
        now_ref[f, r] = now_ref[f, r] * (1.0 / 3.0) + (2.0 / 3.0) * value

    def step(i, carry):
        segment(now_ref, set_one)
        segment(one_ref, set_two)
        segment(two_ref, set_now)
        return carry

    lax.fori_loop(0, STEPS, step, 0)
    for f in range(fields):
        for r in range(total):
            out_ref[f, r] = now_ref[f, r].astype(jnp.bfloat16)


def forecast(block):
    space, fields, rows, local, width = block.shape
    state = (fields, space * rows, local, width)
    return pl.pallas_call(
        forecast_kernel,
        out_shape=jax.ShapeDtypeStruct(state, jnp.bfloat16),
        in_specs=[pl.BlockSpec(memory_space=pltpu.VMEM)],
        out_specs=pl.BlockSpec(memory_space=pltpu.VMEM),
        scratch_shapes=[pltpu.VMEM(state, jnp.float32)] * 3,
    )(block)


def mm(a, b, dims=(((1,), (0,)), ((), ()))):
    return lax.dot_general(a, b, dims, precision=HIGH, preferred_element_type=jnp.float32)


def region_weights(sampled, values, variances):
    members, obs = sampled.shape
    mean_obs = jnp.mean(sampled, axis=0)
    inv = lax.rsqrt(variances)
    basis = (sampled - mean_obs) * inv
    innovation = (values - mean_obs) * inv
    base = members - 1.0
    identity = jnp.eye(obs, dtype=jnp.float32)
    cross = mm(basis, basis, (((0,), (0,)), ((), ())))
    trace = jnp.sum(cross * identity)
    norm_f = jnp.sqrt(members * base * base + 2.0 * base * trace + jnp.sum(cross * cross))
    m = base / norm_f
    l = 1.0
    ym = identity / norm_f
    pm = cross / norm_f + m * identity
    yl = None
    pl_ = None
    for step in range(NS_STEPS):
        s = 1.5 - 0.5 * m
        if step == 0:
            yl, pl_ = -0.5 * ym, 1.5 * identity - 0.5 * pm
        else:
            both = mm(jnp.concatenate([ym, pm]), pl_)
            yl, pl_ = s * yl - 0.5 * both[:obs], 1.5 * pl_ - 0.5 * both[obs:]
        l = s * l
        if step < NS_STEPS - 1:
            square = mm(pm, pm)
            h = (2.25 - 1.5 * m + 0.25 * m * m) * identity + (0.25 * m - 1.5) * pm + 0.25 * square
            both = mm(jnp.concatenate([ym, pm - m * identity]), h)
            m = m * s * s
            ym, pm = both[:obs], both[obs:] + m * identity
    scale = 1.0 / jnp.sqrt(norm_f)
    gain = math.sqrt(base) * scale
    coeff = mm(pl_, mm(pl_, innovation[:, None]))[:, 0] * (scale * scale)
    return basis.astype(jnp.bfloat16), (yl * gain).astype(jnp.bfloat16), coeff, gain * l


def split_pair(x):
    first = lax.reduce_precision(x, 8, 7)
    return first.astype(jnp.bfloat16), (x - first).astype(jnp.bfloat16)


def with_neighbours(block, axis, dim):
    count = lax.axis_size(axis)
    up = [(i, (i + 1) % count) for i in range(count)]
    down = [(j, i) for i, j in up]
    return jnp.concatenate(
        [lax.ppermute(block, axis, up), block, lax.ppermute(block, axis, down)], axis=dim
    )


def blend(deviation, mean, basis, inner, coeff, level, fields, rows, cols):
    members = deviation.shape[0]
    half = rows // 2
    row_weight = jnp.abs((jnp.arange(rows, dtype=jnp.float32) + 0.5) / rows - 0.5)
    col = (jnp.arange(cols, dtype=jnp.float32) + 0.5) / cols - 0.5
    q = jnp.abs(col)
    left = col < 0
    col_terms = (jnp.where(left, q, 0.0), 1.0 - q, jnp.where(left, 0.0, q))
    bands = []
    for row_half in range(2):
        part = slice(row_half * half, (row_half + 1) * half)
        r = row_weight[part]
        picks, factors = [], []
        for row_pick, row_term in ((1, 1.0 - r), (2 * row_half, r)):
            for col_pick in range(3):
                picks.append((row_pick, col_pick))
                factor = row_term[:, None, None] * col_terms[col_pick][None, None, :]
                factors.append(jnp.broadcast_to(factor, (half, fields, cols)).reshape(-1))
        quarter = deviation[:, part].reshape(members, -1)
        stack = jnp.concatenate([basis[p] for p in picks], axis=1)
        seen = lax.dot_general(
            stack, quarter, (((0,), (0,)), ((), ())), preferred_element_type=jnp.float32
        )
        seen = seen.reshape(len(picks), -1, quarter.shape[1])
        turned = lax.dot_general(
            jnp.stack([inner[p] for p in picks]),
            seen.astype(jnp.bfloat16),
            (((2,), (1,)), ((0,), (0,))),
            preferred_element_type=jnp.float32,
        )
        factors = jnp.stack(factors)
        turned = (turned * factors[:, None, :]).astype(jnp.bfloat16)
        shift = jnp.sum(
            jnp.stack([coeff[p] for p in picks])[:, :, None] * seen * factors[:, None, :],
            axis=(0, 1),
        )
        own = jnp.sum(jnp.stack([level[p] for p in picks])[:, None] * factors, axis=0)
        product = lax.dot_general(
            stack,
            turned.reshape(-1, turned.shape[2]),
            (((1,), (0,)), ((), ())),
            preferred_element_type=jnp.float32,
        )
        summed = product + own * quarter.astype(jnp.float32) + (shift + mean[part].reshape(-1))
        bands.append(summed.astype(jnp.bfloat16).reshape(members, half, fields, cols))
    return jnp.concatenate(bands, axis=1)


def per_device(ensemble, obs_index, obs_value, obs_var):
    space = lax.axis_size("space")
    groups = lax.axis_size("member")
    local, fields, rows, width = ensemble.shape[1:]
    regions = obs_index.shape[2]
    cols = width // regions
    members = local * groups
    few = local // space
    both = ("space", "member")
    index = lax.all_gather(obs_index[0, 0], "space", axis=0, tiled=False)
    block = ensemble[0].reshape(space, few, fields, rows, width).transpose(0, 2, 3, 1, 4)
    block = lax.all_to_all(block, "space", split_axis=0, concat_axis=0, tiled=True)
    ahead = forecast(block).reshape(fields, space, rows, few, regions, cols)
    cells = lax.broadcasted_iota(jnp.int32, (rows, cols, index.shape[2]), 0) * cols
    cells = cells + lax.broadcasted_iota(jnp.int32, cells.shape, 1)
    pick = (cells == index[:, :, None, None, :]).astype(jnp.bfloat16)
    picked = jnp.einsum("armbc,abrcp->abmp", ahead[0], pick, preferred_element_type=jnp.float32)
    picked = picked.astype(jnp.bfloat16).reshape(space * regions, few, -1)
    sampled = lax.all_to_all(picked, both, split_axis=0, concat_axis=0, tiled=True)
    sampled = sampled.reshape(members, -1).astype(jnp.float32)
    tile = ahead.transpose(1, 4, 0, 2, 3, 5).reshape(space * regions, fields, rows, few, cols)
    tile = lax.all_to_all(tile, both, split_axis=0, concat_axis=0, tiled=True)

    basis, inner, coeff, level = region_weights(sampled, obs_value[0, 0, 0], obs_var[0, 0, 0])
    basis = with_neighbours(with_neighbours(basis[None, None], "member", 1), "space", 0)
    extra = [p[None] for p in split_pair(coeff)]
    extra += [jnp.broadcast_to(p, extra[0].shape) for p in split_pair(level)]
    pad = jnp.zeros((12,) + coeff.shape, jnp.bfloat16)
    packed = jnp.concatenate([inner] + extra + [pad])[None, None]
    packed = with_neighbours(with_neighbours(packed, "member", 1), "space", 0)
    obs = coeff.shape[0]
    wide = packed[:, :, obs : obs + 4].astype(jnp.float32)

    full = tile.astype(jnp.float32)
    mean = jnp.mean(full, axis=(0, 3))
    deviation = (full - mean[:, :, None, :]).astype(jnp.bfloat16)
    deviation = deviation.transpose(0, 3, 2, 1, 4).reshape(members, rows, fields, cols)
    analysed = blend(
        deviation,
        mean.transpose(1, 0, 2),
        basis,
        packed[:, :, :obs],
        wide[:, :, 0] + wide[:, :, 1],
        wide[:, :, 2, 0] + wide[:, :, 3, 0],
        fields,
        rows,
        cols,
    )
    analysed = analysed.reshape(space, groups, few, rows, fields, cols)
    analysed = analysed.transpose(1, 4, 3, 0, 2, 5).reshape(groups, fields, rows, local, cols)
    returned = lax.all_to_all(analysed, "member", split_axis=0, concat_axis=0, tiled=True)
    return returned.transpose(3, 1, 2, 0, 4).reshape(1, local, fields, rows, width)


def solution(mesh):
    return jax.shard_map(
        per_device,
        mesh=mesh,
        in_specs=(
            P("group", "member", None, "space", None),
            P("group", "space", None, None),
            P("group", "space", "member", None),
            P("group", "space", "member", None),
        ),
        out_specs=P("group", "member", None, "space", None),
        check_vma=False,
    )
```

```python
import functools
import math

import jax
import jax.numpy as jnp
from jax import lax
from jax.experimental import pallas as pl
from jax.experimental.pallas import tpu as pltpu
from jax.sharding import PartitionSpec as P

STEPS = 2
NS_STEPS = 6
TIME_STEP = 0.4
CORIOLIS = 0.3
HIGH = lax.Precision.HIGHEST


def forecast_kernel(block_ref, out_ref, now_ref, one_ref, two_ref):
    space, fields, rows, local, width = block_ref.shape
    total = space * rows

    for f in range(fields):
        for r in range(total):
            now_ref[f, r] = block_ref[r // rows, f, r % rows].astype(jnp.float32)

    def d_col(f):
        return 0.5 * (pltpu.roll(f, width - 1, 1) - pltpu.roll(f, 1, 1))

    def segment(source_ref, combine):
        def row(r, carry):
            up = lax.rem(r + 1, total)
            down = lax.rem(r + total - 1, total)
            h, v, u = source_ref[0, r], source_ref[1, r], source_ref[2, r]
            d_h = -(d_col(u) + 0.5 * (source_ref[1, up] - source_ref[1, down]))
            d_v = -0.5 * (source_ref[0, up] - source_ref[0, down]) - CORIOLIS * u
            d_u = -d_col(h) + CORIOLIS * v
            for f, (value, rate) in enumerate(((h, d_h), (v, d_v), (u, d_u))):
                combine(f, r, value + TIME_STEP * rate)
            return carry

        lax.fori_loop(0, total, row, 0)

    def set_one(f, r, value):
        one_ref[f, r] = value

    def set_two(f, r, value):
        two_ref[f, r] = 0.75 * now_ref[f, r] + 0.25 * value

    def set_now(f, r, value):
        now_ref[f, r] = now_ref[f, r] * (1.0 / 3.0) + (2.0 / 3.0) * value

    def step(i, carry):
        segment(now_ref, set_one)
        segment(one_ref, set_two)
        segment(two_ref, set_now)
        return carry

    lax.fori_loop(0, STEPS, step, 0)
    for f in range(fields):
        for r in range(total):
            out_ref[f, r] = now_ref[f, r].astype(jnp.bfloat16)


def forecast(block):
    space, fields, rows, local, width = block.shape
    state = (fields, space * rows, local, width)
    return pl.pallas_call(
        forecast_kernel,
        out_shape=jax.ShapeDtypeStruct(state, jnp.bfloat16),
        in_specs=[pl.BlockSpec(memory_space=pltpu.VMEM)],
        out_specs=pl.BlockSpec(memory_space=pltpu.VMEM),
        scratch_shapes=[pltpu.VMEM(state, jnp.float32)] * 3,
    )(block)


def mm(a, b, dims=(((1,), (0,)), ((), ()))):
    return lax.dot_general(a, b, dims, precision=HIGH, preferred_element_type=jnp.float32)


def eye_of(n):
    shape = (n, n)
    same = lax.broadcasted_iota(jnp.int32, shape, 0) == lax.broadcasted_iota(jnp.int32, shape, 1)
    return same.astype(jnp.float32)


def total(x):
    return jnp.sum(jnp.sum(x, axis=0, keepdims=True), axis=1, keepdims=True)


EXTRA = 16


def weights_kernel(sampled_ref, values_ref, variances_ref, out_ref):
    sampled = sampled_ref[...].astype(jnp.float32)
    members, obs = sampled.shape
    mean_obs = jnp.sum(sampled, axis=0, keepdims=True) * (1.0 / members)
    inv = lax.rsqrt(variances_ref[...])
    basis = (sampled - mean_obs) * inv
    out_ref[0:members] = basis.astype(jnp.bfloat16)
    innovation = (values_ref[...] - mean_obs) * inv
    base = members - 1.0
    identity = eye_of(obs)
    cross = mm(basis, basis, (((0,), (0,)), ((), ())))
    trace = total(cross * identity)
    norm_f = jnp.sqrt(members * base * base + 2.0 * base * trace + total(cross * cross))
    m = base / norm_f
    ym = identity / norm_f
    pm = cross / norm_f + m * identity
    yl, pl_, l = None, None, 1.0
    for step in range(NS_STEPS):
        s = 1.5 - 0.5 * m
        if step == 0:
            yl, pl_ = -0.5 * ym, 1.5 * identity - 0.5 * pm
        else:
            yl, pl_ = s * yl - 0.5 * mm(ym, pl_), 1.5 * pl_ - 0.5 * mm(pm, pl_)
        l = s * l
        if step < NS_STEPS - 1:
            square = mm(pm, pm)
            h = (2.25 - 1.5 * m + 0.25 * m * m) * identity + (0.25 * m - 1.5) * pm + 0.25 * square
            shifted = pm - m * identity
            m = m * s * s
            ym, pm = mm(ym, h), mm(shifted, h) + m * identity
    scale = lax.rsqrt(norm_f)
    gain = math.sqrt(base) * scale
    row = jnp.broadcast_to(innovation, (EXTRA, obs))
    coeff = mm(mm(row, pl_), pl_) * (scale * scale)
    out_ref[members : members + obs] = (yl * gain).astype(jnp.bfloat16)
    which = lax.broadcasted_iota(jnp.int32, (EXTRA, obs), 0)
    wide = jnp.where(which < 2, coeff, gain * l)
    first = wide.astype(jnp.bfloat16).astype(jnp.float32)
    extra = jnp.where(which % 2 == 0, first, wide - first)
    out_ref[members + obs :] = extra.astype(jnp.bfloat16)


def region_weights(sampled, values, variances):
    members, obs = sampled.shape
    return pl.pallas_call(
        weights_kernel,
        out_shape=jax.ShapeDtypeStruct((members + obs + EXTRA, obs), jnp.bfloat16),
        in_specs=[pl.BlockSpec(memory_space=pltpu.VMEM)] * 3,
        out_specs=pl.BlockSpec(memory_space=pltpu.VMEM),
    )(sampled, values[None], variances[None])


def exchange_kernel(groups, space, own_ref, out_ref, keep_sem, send_sem, recv_sem):
    m, s = lax.axis_index("member"), lax.axis_index("space")
    right, left = lax.rem(m + 1, groups), lax.rem(m + groups - 1, groups)
    odd = lax.rem(s, 2)
    partner = s + 1 - 2 * odd
    far = lax.rem(s + 2 - 4 * odd + space, space)
    source = lax.rem(s - 2 + 4 * odd + space, space)
    mesh_id = pl.DeviceIdType.MESH
    barrier = pltpu.get_barrier_semaphore()
    for device in (
        {"member": right},
        {"member": left},
        {"space": partner},
        {"space": far},
        {"space": source},
    ):
        pl.semaphore_signal(barrier, inc=1, device_id=device, device_id_type=mesh_id)
    pl.semaphore_wait(barrier, 5)

    def copy(i, src, dst, device):
        made = pltpu.make_async_remote_copy(
            src_ref=src,
            dst_ref=dst,
            send_sem=send_sem.at[i],
            recv_sem=recv_sem.at[i],
            device_id=device,
            device_id_type=mesh_id,
        )
        made.start()
        return made

    put, got = 2 * odd, 2 - 2 * odd
    z_up = copy(0, own_ref, out_ref.at[1, 0], {"member": right})
    z_down = copy(1, own_ref, out_ref.at[1, 2], {"member": left})
    x_own = copy(2, own_ref, out_ref.at[put, 1], {"space": partner})
    keep = pltpu.make_async_copy(own_ref, out_ref.at[1, 1], keep_sem)
    keep.start()
    x_own.wait_recv()
    f_own = copy(5, out_ref.at[got, 1], out_ref.at[put, 1], {"space": far})
    z_up.wait_recv()
    x_up = copy(3, out_ref.at[1, 0], out_ref.at[put, 0], {"space": partner})
    z_down.wait_recv()
    x_down = copy(4, out_ref.at[1, 2], out_ref.at[put, 2], {"space": partner})
    x_up.wait_recv()
    f_up = copy(6, out_ref.at[got, 0], out_ref.at[put, 0], {"space": far})
    x_down.wait_recv()
    f_down = copy(7, out_ref.at[got, 2], out_ref.at[put, 2], {"space": far})
    keep.wait()
    for made in (f_own, f_up, f_down):
        made.wait_recv()
    for made in (z_up, z_down, x_own, x_up, x_down, f_own, f_up, f_down):
        made.wait_send()


def neighbours(own):
    groups, space = lax.axis_size("member"), lax.axis_size("space")
    return pl.pallas_call(
        functools.partial(exchange_kernel, groups, space),
        out_shape=jax.ShapeDtypeStruct((3, 3) + own.shape, own.dtype),
        in_specs=[pl.BlockSpec(memory_space=pltpu.VMEM)],
        out_specs=pl.BlockSpec(memory_space=pltpu.VMEM),
        scratch_shapes=[
            pltpu.SemaphoreType.DMA,
            pltpu.SemaphoreType.DMA((8,)),
            pltpu.SemaphoreType.DMA((8,)),
        ],
        compiler_params=pltpu.CompilerParams(collective_id=0, has_side_effects=True),
    )(own)


def blend_kernel(members_ref, nine_ref, factor_ref, out_ref, acc_ref):
    half = pl.program_id(0)
    members = members_ref.shape[0]
    obs = nine_ref.shape[3]
    full = members_ref[...].astype(jnp.float32)
    mean = jnp.sum(full, axis=0, keepdims=True) * (1.0 / members)
    deviation = (full - mean).astype(jnp.bfloat16)
    own = jnp.zeros_like(mean)
    shift = mean
    for t in range(6):
        row_pick = 1 if t < 3 else 2 * half
        col_pick = t % 3
        factor = factor_ref[0, t : t + 1]
        basis = nine_ref[row_pick, col_pick, 0:members]
        inner = nine_ref[row_pick, col_pick, members : members + obs]
        extra = nine_ref[row_pick, col_pick, members + obs :]
        seen = lax.dot_general(
            basis, deviation, (((0,), (0,)), ((), ())), preferred_element_type=jnp.float32
        ).astype(jnp.bfloat16)
        turned = jnp.dot(inner, seen, preferred_element_type=jnp.float32)
        centre = jnp.dot(extra, seen, preferred_element_type=jnp.float32)
        shift = shift + factor * (centre[0:1] + centre[1:2])
        level = extra.astype(jnp.float32)
        own = own + factor * (level[2:3, 0:1] + level[3:4, 0:1])
        part = jnp.dot(
            basis, (turned * factor).astype(jnp.bfloat16), preferred_element_type=jnp.float32
        )
        if t == 0:
            acc_ref[...] = part
        else:
            acc_ref[...] += part
    deviation = (members_ref[...].astype(jnp.float32) - mean).astype(jnp.bfloat16)
    out_ref[...] = (acc_ref[...] + own * deviation.astype(jnp.float32) + shift).astype(jnp.bfloat16)


def blend(region, nine, fields, rows, cols):
    members = region.shape[0]
    half = rows // 2
    row_weight = jnp.abs((jnp.arange(rows, dtype=jnp.float32) + 0.5) / rows - 0.5)
    col = (jnp.arange(cols, dtype=jnp.float32) + 0.5) / cols - 0.5
    q = jnp.abs(col)
    col_terms = jnp.stack([jnp.where(col < 0, q, 0.0), 1.0 - q, jnp.where(col < 0, 0.0, q)])
    row_terms = jnp.stack([1.0 - row_weight, row_weight]).reshape(2, 2, half).transpose(1, 0, 2)
    factors = row_terms[:, :, None, :, None, None] * col_terms[None, None, :, None, None, :]
    factors = jnp.broadcast_to(factors, (2, 2, 3, half, fields, cols)).reshape(2, 6, -1)
    span = half * fields * cols
    return pl.pallas_call(
        blend_kernel,
        grid=(2,),
        out_shape=jax.ShapeDtypeStruct(region.shape, jnp.bfloat16),
        in_specs=[
            pl.BlockSpec((members, span), lambda i: (0, i)),
            pl.BlockSpec(nine.shape, lambda i: (0, 0, 0, 0)),
            pl.BlockSpec((1, 6, span), lambda i: (i, 0, 0)),
        ],
        out_specs=pl.BlockSpec((members, span), lambda i: (0, i)),
        scratch_shapes=[pltpu.VMEM((members, span), jnp.float32)],
    )(region, nine, factors)


def per_device(ensemble, obs_index, obs_value, obs_var):
    space = lax.axis_size("space")
    groups = lax.axis_size("member")
    local, fields, rows, width = ensemble.shape[1:]
    regions = obs_index.shape[2]
    cols = width // regions
    members = local * groups
    few = local // space
    both = ("space", "member")
    index = lax.all_gather(obs_index[0, 0], "space", axis=0, tiled=False)
    block = ensemble[0].reshape(space, few, fields, rows, width).transpose(0, 2, 3, 1, 4)
    block = lax.all_to_all(block, "space", split_axis=0, concat_axis=0, tiled=True)
    ahead = forecast(block).reshape(fields, space, rows, few, regions, cols)
    cells = lax.broadcasted_iota(jnp.int32, (rows, cols, index.shape[2]), 0) * cols
    cells = cells + lax.broadcasted_iota(jnp.int32, cells.shape, 1)
    pick = (cells == index[:, :, None, None, :]).astype(jnp.bfloat16)
    picked = jnp.einsum("armbc,abrcp->abmp", ahead[0], pick, preferred_element_type=jnp.float32)
    picked = picked.astype(jnp.bfloat16).reshape(space * regions, few, -1)
    sampled = lax.all_to_all(picked, both, split_axis=0, concat_axis=0, tiled=True)
    sampled = sampled.reshape(members, -1)
    tile = ahead.transpose(1, 4, 0, 2, 3, 5).reshape(space * regions, fields, rows, few, cols)
    tile = lax.all_to_all(tile, both, split_axis=0, concat_axis=0, tiled=True)

    own = region_weights(sampled, obs_value[0, 0, 0], obs_var[0, 0, 0])
    nine = neighbours(own)
    region = tile.transpose(0, 3, 2, 1, 4).reshape(members, rows * fields * cols)
    analysed = blend(region, nine, fields, rows, cols)
    analysed = analysed.reshape(space, groups, few, rows, fields, cols)
    analysed = analysed.transpose(1, 4, 3, 0, 2, 5).reshape(groups, fields, rows, local, cols)
    returned = lax.all_to_all(analysed, "member", split_axis=0, concat_axis=0, tiled=True)
    return returned.transpose(3, 1, 2, 0, 4).reshape(1, local, fields, rows, width)


def solution(mesh):
    return jax.shard_map(
        per_device,
        mesh=mesh,
        in_specs=(
            P("group", "member", None, "space", None),
            P("group", "space", None, None),
            P("group", "space", "member", None),
            P("group", "space", "member", None),
        ),
        out_specs=P("group", "member", None, "space", None),
        check_vma=False,
    )
```

```python
import functools
import math

import jax
import jax.numpy as jnp
from jax import lax
from jax.experimental import pallas as pl
from jax.experimental.pallas import tpu as pltpu
from jax.sharding import PartitionSpec as P


STEPS = 2
NS_STEPS = 6
TIME_STEP = 0.4
CORIOLIS = 0.3
HIGH = lax.Precision.HIGHEST


def forecast_kernel(block_ref, out_ref, now_ref, one_ref, two_ref):
    space, fields, rows, _, width = block_ref.shape
    total = space * rows

    for f in range(fields):
        for r in range(total):
            now_ref[f, r] = block_ref[r // rows, f, r % rows].astype(jnp.float32)

    def d_col(f):
        return 0.5 * (pltpu.roll(f, width - 1, 1) - pltpu.roll(f, 1, 1))

    def segment(source_ref, combine):
        def row(r, carry):
            up = lax.rem(r + 1, total)
            down = lax.rem(r + total - 1, total)
            h, v, u = source_ref[0, r], source_ref[1, r], source_ref[2, r]
            d_h = -(d_col(u) + 0.5 * (source_ref[1, up] - source_ref[1, down]))
            d_v = -0.5 * (source_ref[0, up] - source_ref[0, down]) - CORIOLIS * u
            d_u = -d_col(h) + CORIOLIS * v
            for f, (value, rate) in enumerate(((h, d_h), (v, d_v), (u, d_u))):
                combine(f, r, value + TIME_STEP * rate)
            return carry

        lax.fori_loop(0, total, row, 0)

    def set_one(f, r, value):
        one_ref[f, r] = value

    def set_two(f, r, value):
        two_ref[f, r] = 0.75 * now_ref[f, r] + 0.25 * value

    def set_now(f, r, value):
        now_ref[f, r] = now_ref[f, r] * (1.0 / 3.0) + (2.0 / 3.0) * value

    def step(i, carry):
        segment(now_ref, set_one)
        segment(one_ref, set_two)
        segment(two_ref, set_now)
        return carry

    lax.fori_loop(0, STEPS, step, 0)
    for f in range(fields):
        for r in range(total):
            out_ref[f, r] = now_ref[f, r].astype(jnp.bfloat16)


def forecast(block):
    space, fields, rows, local, width = block.shape
    state = (fields, space * rows, local, width)
    return pl.pallas_call(
        forecast_kernel,
        out_shape=jax.ShapeDtypeStruct(state, jnp.bfloat16),
        in_specs=[pl.BlockSpec(memory_space=pltpu.VMEM)],
        out_specs=pl.BlockSpec(memory_space=pltpu.VMEM),
        scratch_shapes=[pltpu.VMEM(state, jnp.float32)] * 3,
    )(block)


def mm(a, b, dims=(((1,), (0,)), ((), ()))):
    return lax.dot_general(a, b, dims, precision=HIGH, preferred_element_type=jnp.float32)


def eye_of(n):
    shape = (n, n)
    same = lax.broadcasted_iota(jnp.int32, shape, 0) == lax.broadcasted_iota(jnp.int32, shape, 1)
    return same.astype(jnp.float32)


def total(x):
    return jnp.sum(jnp.sum(x, axis=0, keepdims=True), axis=1, keepdims=True)


EXTRA = 16


def weights_kernel(sampled_ref, values_ref, variances_ref, out_ref):
    sampled = sampled_ref[...].astype(jnp.float32)
    members, obs = sampled.shape
    mean_obs = jnp.sum(sampled, axis=0, keepdims=True) * (1.0 / members)
    inv = lax.rsqrt(variances_ref[...])
    basis = (sampled - mean_obs) * inv
    out_ref[0:members] = basis.astype(jnp.bfloat16)
    innovation = (values_ref[...] - mean_obs) * inv
    base = members - 1.0
    identity = eye_of(obs)
    cross = mm(basis, basis, (((0,), (0,)), ((), ())))
    trace = total(cross * identity)
    norm_f = jnp.sqrt(members * base * base + 2.0 * base * trace + total(cross * cross))
    m = base / norm_f
    ym = identity / norm_f
    pm = cross / norm_f + m * identity
    yl, pl_, l = None, None, 1.0
    for step in range(NS_STEPS):
        s = 1.5 - 0.5 * m
        if step == 0:
            yl, pl_ = -0.5 * ym, 1.5 * identity - 0.5 * pm
        else:
            yl, pl_ = s * yl - 0.5 * mm(ym, pl_), 1.5 * pl_ - 0.5 * mm(pm, pl_)
        l = s * l
        if step < NS_STEPS - 1:
            square = mm(pm, pm)
            h = (2.25 - 1.5 * m + 0.25 * m * m) * identity + (0.25 * m - 1.5) * pm + 0.25 * square
            shifted = pm - m * identity
            m = m * s * s
            ym, pm = mm(ym, h), mm(shifted, h) + m * identity
    scale = lax.rsqrt(norm_f)
    gain = math.sqrt(base) * scale
    row = jnp.broadcast_to(innovation, (EXTRA, obs))
    coeff = mm(mm(row, pl_), pl_) * (scale * scale)
    out_ref[members : members + obs] = (yl * gain).astype(jnp.bfloat16)
    which = lax.broadcasted_iota(jnp.int32, (EXTRA, obs), 0)
    wide = jnp.where(which < 2, coeff, gain * l)
    first = wide.astype(jnp.bfloat16).astype(jnp.float32)
    extra = jnp.where(which % 2 == 0, first, wide - first)
    out_ref[members + obs :] = extra.astype(jnp.bfloat16)


def region_weights(sampled, values, variances):
    members, obs = sampled.shape
    return pl.pallas_call(
        weights_kernel,
        out_shape=jax.ShapeDtypeStruct((members + obs + EXTRA, obs), jnp.bfloat16),
        in_specs=[pl.BlockSpec(memory_space=pltpu.VMEM)] * 3,
        out_specs=pl.BlockSpec(memory_space=pltpu.VMEM),
    )(sampled, values[None], variances[None])


def deal_kernel(groups, space, picked_ref, out_ref, keep_sem, send_sem, recv_sem):
    m, s = lax.axis_index("member"), lax.axis_index("space")
    count = groups * space
    me = m * space + s
    mesh_id = pl.DeviceIdType.MESH

    def place(index):
        return {"member": index // space, "space": lax.rem(index, space)}

    barrier = pltpu.get_barrier_semaphore()
    for d in range(1, count):
        pl.semaphore_signal(
            barrier, inc=1, device_id=place(lax.rem(me + d, count)), device_id_type=mesh_id
        )
    pl.semaphore_wait(barrier, count - 1)
    keep = pltpu.make_async_copy(picked_ref.at[me], out_ref.at[me], keep_sem)
    keep.start()
    started = [keep]
    for d in range(1, count):
        to = lax.rem(me + d, count)
        made = pltpu.make_async_remote_copy(
            src_ref=picked_ref.at[to],
            dst_ref=out_ref.at[me],
            send_sem=send_sem.at[d - 1],
            recv_sem=recv_sem.at[d - 1],
            device_id=place(to),
            device_id_type=mesh_id,
        )
        made.start()
        started.append(made)
    for made in started:
        made.wait()


def deal(picked):
    groups, space = lax.axis_size("member"), lax.axis_size("space")
    vmem = pl.BlockSpec(memory_space=pltpu.VMEM)
    return pl.pallas_call(
        functools.partial(deal_kernel, groups, space),
        out_shape=jax.ShapeDtypeStruct(picked.shape, picked.dtype),
        in_specs=[vmem],
        out_specs=vmem,
        scratch_shapes=[
            pltpu.SemaphoreType.DMA,
            pltpu.SemaphoreType.DMA((groups * space - 1,)),
            pltpu.SemaphoreType.DMA((groups * space - 1,)),
        ],
        compiler_params=pltpu.CompilerParams(collective_id=2, has_side_effects=True),
    )(picked)


def exchange_kernel(groups, space, own_ref, out_ref, keep_sem, send_sem, recv_sem):
    m, s = lax.axis_index("member"), lax.axis_index("space")
    right, left = lax.rem(m + 1, groups), lax.rem(m + groups - 1, groups)
    odd = lax.rem(s, 2)
    partner = s + 1 - 2 * odd
    far = lax.rem(s + 2 - 4 * odd + space, space)
    source = lax.rem(s - 2 + 4 * odd + space, space)
    mesh_id = pl.DeviceIdType.MESH
    barrier = pltpu.get_barrier_semaphore()
    for device in (
        {"member": right},
        {"member": left},
        {"space": partner},
        {"space": far},
        {"space": source},
    ):
        pl.semaphore_signal(barrier, inc=1, device_id=device, device_id_type=mesh_id)
    pl.semaphore_wait(barrier, 5)

    def copy(i, src, dst, device):
        made = pltpu.make_async_remote_copy(
            src_ref=src,
            dst_ref=dst,
            send_sem=send_sem.at[i],
            recv_sem=recv_sem.at[i],
            device_id=device,
            device_id_type=mesh_id,
        )
        made.start()
        return made

    put, got = 2 * odd, 2 - 2 * odd
    z_up = copy(0, own_ref, out_ref.at[1, 0], {"member": right})
    z_down = copy(1, own_ref, out_ref.at[1, 2], {"member": left})
    x_own = copy(2, own_ref, out_ref.at[put, 1], {"space": partner})
    keep = pltpu.make_async_copy(own_ref, out_ref.at[1, 1], keep_sem)
    keep.start()
    x_own.wait_recv()
    f_own = copy(5, out_ref.at[got, 1], out_ref.at[put, 1], {"space": far})
    z_up.wait_recv()
    x_up = copy(3, out_ref.at[1, 0], out_ref.at[put, 0], {"space": partner})
    z_down.wait_recv()
    x_down = copy(4, out_ref.at[1, 2], out_ref.at[put, 2], {"space": partner})
    x_up.wait_recv()
    f_up = copy(6, out_ref.at[got, 0], out_ref.at[put, 0], {"space": far})
    x_down.wait_recv()
    f_down = copy(7, out_ref.at[got, 2], out_ref.at[put, 2], {"space": far})
    keep.wait()
    for made in (f_own, f_up, f_down):
        made.wait_recv()
    for made in (z_up, z_down, x_own, x_up, x_down, f_own, f_up, f_down):
        made.wait_send()


def neighbours(own):
    groups, space = lax.axis_size("member"), lax.axis_size("space")
    return pl.pallas_call(
        functools.partial(exchange_kernel, groups, space),
        out_shape=jax.ShapeDtypeStruct((3, 3) + own.shape, own.dtype),
        in_specs=[pl.BlockSpec(memory_space=pltpu.VMEM)],
        out_specs=pl.BlockSpec(memory_space=pltpu.VMEM),
        scratch_shapes=[
            pltpu.SemaphoreType.DMA,
            pltpu.SemaphoreType.DMA((8,)),
            pltpu.SemaphoreType.DMA((8,)),
        ],
        compiler_params=pltpu.CompilerParams(collective_id=0, has_side_effects=True),
    )(own)


def blend_half(half, members_ref, nine_ref, factor_ref, acc_ref):
    members = members_ref.shape[0]
    obs = nine_ref.shape[3]
    span = factor_ref.shape[2]
    part_of = slice(half * span, (half + 1) * span)
    full = members_ref[:, part_of].astype(jnp.float32)
    mean = jnp.sum(full, axis=0, keepdims=True) * (1.0 / members)
    deviation = (full - mean).astype(jnp.bfloat16)
    own = jnp.zeros_like(mean)
    shift = mean
    for t in range(6):
        row_pick = 1 if t < 3 else 2 * half
        col_pick = t % 3
        factor = factor_ref[half, t : t + 1]
        basis = nine_ref[row_pick, col_pick, 0:members]
        inner = nine_ref[row_pick, col_pick, members : members + obs]
        extra = nine_ref[row_pick, col_pick, members + obs :]
        seen = lax.dot_general(
            basis, deviation, (((0,), (0,)), ((), ())), preferred_element_type=jnp.float32
        ).astype(jnp.bfloat16)
        turned = jnp.dot(inner, seen, preferred_element_type=jnp.float32)
        centre = jnp.dot(extra, seen, preferred_element_type=jnp.float32)
        shift = shift + factor * (centre[0:1] + centre[1:2])
        level = extra.astype(jnp.float32)
        own = own + factor * (level[2:3, 0:1] + level[3:4, 0:1])
        part = jnp.dot(
            basis, (turned * factor).astype(jnp.bfloat16), preferred_element_type=jnp.float32
        )
        if t == 0:
            acc_ref[...] = part
        else:
            acc_ref[...] += part
    deviation = (members_ref[:, part_of].astype(jnp.float32) - mean).astype(jnp.bfloat16)
    return (acc_ref[...] + own * deviation.astype(jnp.float32) + shift).astype(jnp.bfloat16)


def blend_kernel(
    groups, members_ref, nine_ref, factor_ref, out_ref, acc_ref, mine_ref, keep_sem, send_sem, recv_sem
):
    m = lax.axis_index("member")
    mesh_id = pl.DeviceIdType.MESH
    local = out_ref.shape[2]
    barrier = pltpu.get_barrier_semaphore()
    for d in range(1, groups):
        pl.semaphore_signal(
            barrier, inc=1, device_id={"member": lax.rem(m + d, groups)}, device_id_type=mesh_id
        )
    started = []
    for half in range(2):
        mine_ref[half] = blend_half(half, members_ref, nine_ref, factor_ref, acc_ref)
        if half == 0:
            pl.semaphore_wait(barrier, groups - 1)
        here = pl.ds(pl.multiple_of(m * local, local), local)
        keep = pltpu.make_async_copy(
            mine_ref.at[half, here], out_ref.at[m, half], keep_sem.at[half]
        )
        keep.start()
        started.append(keep)
        for d in range(1, groups):
            to = lax.rem(m + d, groups)
            rows = pl.ds(pl.multiple_of(to * local, local), local)
            made = pltpu.make_async_remote_copy(
                src_ref=mine_ref.at[half, rows],
                dst_ref=out_ref.at[m, half],
                send_sem=send_sem.at[half, d - 1],
                recv_sem=recv_sem.at[half, d - 1],
                device_id={"member": to},
                device_id_type=mesh_id,
            )
            made.start()
            started.append(made)
    for made in started:
        made.wait()


def blend(region, nine, fields, rows, cols):
    members = region.shape[0]
    half = rows // 2
    row_weight = jnp.abs((jnp.arange(rows, dtype=jnp.float32) + 0.5) / rows - 0.5)
    col = (jnp.arange(cols, dtype=jnp.float32) + 0.5) / cols - 0.5
    q = jnp.abs(col)
    col_terms = jnp.stack([jnp.where(col < 0, q, 0.0), 1.0 - q, jnp.where(col < 0, 0.0, q)])
    row_terms = jnp.stack([1.0 - row_weight, row_weight]).reshape(2, 2, half).transpose(1, 0, 2)
    factors = row_terms[:, :, None, :, None, None] * col_terms[None, None, :, None, None, :]
    factors = jnp.broadcast_to(factors, (2, 2, 3, half, fields, cols)).reshape(2, 6, -1)
    span = half * fields * cols
    groups = lax.axis_size("member")
    vmem = pl.BlockSpec(memory_space=pltpu.VMEM)
    return pl.pallas_call(
        functools.partial(blend_kernel, groups),
        out_shape=jax.ShapeDtypeStruct((groups, 2, members // groups, span), jnp.bfloat16),
        in_specs=[vmem] * 3,
        out_specs=vmem,
        scratch_shapes=[
            pltpu.VMEM((members, span), jnp.float32),
            pltpu.VMEM((2, members, span), jnp.bfloat16),
            pltpu.SemaphoreType.DMA((2,)),
            pltpu.SemaphoreType.DMA((2, groups - 1)),
            pltpu.SemaphoreType.DMA((2, groups - 1)),
        ],
        compiler_params=pltpu.CompilerParams(collective_id=1, has_side_effects=True),
    )(region, nine, factors)


def per_device(ensemble, obs_index, obs_value, obs_var):
    space = lax.axis_size("space")
    groups = lax.axis_size("member")
    local, fields, rows, width = ensemble.shape[1:]
    regions = obs_index.shape[2]
    cols = width // regions
    members = local * groups
    few = local // space
    both = ("member", "space")
    index = lax.all_gather(obs_index[0, 0], "space", axis=0, tiled=False)
    block = ensemble[0].reshape(space, few, fields, rows, width).transpose(0, 2, 3, 1, 4)
    block = lax.all_to_all(block, "space", split_axis=0, concat_axis=0, tiled=True)
    ahead = forecast(block).reshape(fields, space, rows, few, regions, cols)
    cells = lax.broadcasted_iota(jnp.int32, (rows, cols, index.shape[2]), 0) * cols
    cells = cells + lax.broadcasted_iota(jnp.int32, cells.shape, 1)
    pick = (cells == index[:, :, None, None, :]).astype(jnp.bfloat16)
    picked = jnp.einsum("armbc,abrcp->bamp", ahead[0], pick, preferred_element_type=jnp.float32)
    picked = picked.astype(jnp.bfloat16).reshape(space * regions, few, -1)
    sampled = deal(picked)
    sampled = sampled.reshape(members, -1)
    tile = ahead.transpose(4, 1, 2, 0, 3, 5).reshape(space * regions, rows, fields, few, cols)
    sampled, tile = lax.optimization_barrier((sampled, tile))
    tile = lax.all_to_all(tile, both, split_axis=0, concat_axis=0, tiled=True)

    own = region_weights(sampled, obs_value[0, 0, 0], obs_var[0, 0, 0])
    nine = neighbours(own)
    region = tile.transpose(0, 3, 1, 2, 4).reshape(members, rows * fields * cols)
    analysed = blend(region, nine, fields, rows, cols)
    analysed = analysed.reshape(groups, 2, local, rows // 2, fields, cols)
    return analysed.transpose(2, 4, 1, 3, 0, 5).reshape(1, local, fields, rows, width)


def solution(mesh):
    return jax.shard_map(
        per_device,
        mesh=mesh,
        in_specs=(
            P("group", "member", None, "space", None),
            P("group", "space", None, None),
            P("group", "space", "member", None),
            P("group", "space", "member", None),
        ),
        out_specs=P("group", "member", None, "space", None),
        check_vma=False,
    )
```
